512 devices in a mesh: tgt: 16 (over y, x_lo, core), src: 32 (over z, x_hi).
Axes of the slice: x: 4 (x_hi: 2, x_lo: 2; x = x_hi * 2 + x_lo), y: 4, z: 16, core: 2. Of those that a mesh axis runs over, the one named last changes fastest.
Arguments:
- shear_leaves: bfloat16 [32, 32, 128, 128], P('tgt', 'src'), may hold values from -2 to 2, as said below
- normal_leaves: bfloat16 [32, 32, 128, 128], P('tgt', 'src'), may hold values from -2 to 2, as said below
- near_flags: int32 [32, 32], P('tgt', 'src'), may hold values from 0 to 1, as said below
- ranks: int32 [32, 32], P('tgt', 'src'), may hold values from 16 to 64
- shear_traction: float32 [4096, 128], P(('tgt', 'src')), may hold values from -1 to 1
- normal_traction: float32 [4096, 128], P(('tgt', 'src')), may hold values from 0.5 to 4
- state: float32 [4096, 128], P(('tgt', 'src')), may hold values from -0.5 to 0.5
- friction_a: float32 [4096, 128], P(('tgt', 'src')), may hold values from 1 to 2
- heal_rate: float32 [4096, 128], P(('tgt', 'src')), may hold values from 0.1 to 0.5
Outputs:
- shear_out: float32 [4096, 128], P(('tgt', 'src'))
- normal_out: float32 [4096, 128], P(('tgt', 'src'))
- state_out: float32 [4096, 128], P(('tgt', 'src'))
The draws below stay inside these ranges and needn't reach their ends.
Inputs may be any that keep to these rules, and one draw needn't show every extreme that they name: `near_flags`: every leaf with equal leaf row and leaf column is 1, and a 1 stands only where the leaf row and the leaf column differ by at most 1. `shear_leaves`: columns 0 to 63 of an admissible leaf hold its factor U, columns 64 onward its factor V. `normal_leaves`: columns 0 to 63 of an admissible leaf hold its factor U, columns 64 onward its factor V.
All inputs are finite; a program needn't handle non-finite values.
Results may differ from the reference program's by a relative error of at most 0.002.
Values may be sent and summed in bfloat16 or wider, within the bound.
A program may use at most 64 MiB of HBM per device.

```python
import math
import jax
import jax.numpy as jnp
from jax import lax

RMAX = 64
BLK = 128
NV = 128
LEAVES = 32
ELEMENTS = 4096


def leaf_pattern(key):
    coin_bits = jax.random.randint(jax.random.fold_in(key, 7), (LEAVES, LEAVES), 0, 2)
    row_ids = jnp.arange(LEAVES, dtype=jnp.int32)[:, None]
    col_ids = jnp.arange(LEAVES, dtype=jnp.int32)[None, :]
    spacing = jnp.abs(row_ids - col_ids)
    chosen = (spacing == 0) | (spacing == 1) & (coin_bits == 1)
    return jnp.where(chosen, 1, 0).astype(jnp.int32)


def leaf_values(key, salt, self_term):
    pattern = leaf_pattern(key)
    shape = (LEAVES, LEAVES, BLK, BLK)
    raw = jax.random.normal(jax.random.fold_in(key, salt), shape, jnp.float32)
    dense_scale = 0.5 / math.sqrt(BLK)
    factor_scale = (2.25 / (RMAX * BLK * LEAVES)) ** 0.25
    scaling = jnp.where(pattern[:, :, None, None] == 1, dense_scale, factor_scale).astype(jnp.float32)
    same_leaf = (jnp.arange(LEAVES)[:, None] == jnp.arange(LEAVES)[None, :]).astype(jnp.float32)
    values = raw * scaling + self_term * same_leaf[:, :, None, None] * jnp.eye(BLK, dtype=jnp.float32)[None, None]
    return values.astype(jnp.bfloat16)


def draw_near_flags(key, part):
    return leaf_pattern(key)


def draw_shear_leaves(key, part):
    return leaf_values(key, 21, -1.0)


def draw_normal_leaves(key, part):
    return leaf_values(key, 22, 0.0)


def set_ends(array, own_key, least, top_value):
    longest = array.shape.index(max(array.shape))
    spots = []
    for shift in (0, 1):
        where = [jax.random.randint(jax.random.fold_in(own_key, axis), (), 0, length) for axis, length in enumerate(array.shape)]
        where[longest] = (where[longest] + shift) % array.shape[longest]
        spots.append(tuple(where))
    return array.at[spots[0]].set(least).at[spots[1]].set(top_value)


def level_of(rng, extent, split, smallest, top_value):
    def one(dim, blocks):
        draws = jax.random.uniform(jax.random.fold_in(jax.random.fold_in(rng, 6), dim), (blocks,), jnp.float32, smallest / len(split), top_value / len(split))
        return jnp.repeat(jnp.exp(draws), extent[dim] // blocks).reshape((-1,) + (1,) * (len(extent) - dim - 1))

    level = one(*split[0])
    for cut in split[1:]:
        level = level * one(*cut)
    return level


def setup_inputs(seed: int = 0) -> dict:
    key_of = jax.random.split(jax.random.key(seed), 10)
    return {
        "shear_leaves": draw_shear_leaves(jax.random.fold_in(key_of[9], 71), 0),
        "normal_leaves": draw_normal_leaves(jax.random.fold_in(key_of[9], 71), 0),
        "near_flags": draw_near_flags(jax.random.fold_in(key_of[9], 71), 0),
        "ranks": set_ends(jax.random.randint(key_of[3], (LEAVES, LEAVES), RMAX // 4, RMAX + 1), jax.random.fold_in(key_of[3], 1), RMAX // 4, RMAX).astype(jnp.int32),
        "shear_traction": jnp.clip(jax.random.uniform(key_of[4], (ELEMENTS, NV), jnp.float32, -1.0, 1.0) * level_of(key_of[4], (ELEMENTS, NV), ((0, 512),), -0.4, 0.0), -1.0, 1.0),
        "normal_traction": jnp.clip(jnp.exp(math.log(4.0) - 2.0794415 * jax.random.uniform(key_of[5], (ELEMENTS, NV), jnp.float32) ** level_of(key_of[5], (ELEMENTS, NV), ((0, 512),), -0.2, 0.2)), 0.5, 4.0),
        "state": jnp.clip(jax.random.uniform(key_of[6], (ELEMENTS, NV), jnp.float32, -0.5, 0.5) * level_of(key_of[6], (ELEMENTS, NV), ((0, 512),), -0.4, 0.0), -0.5, 0.5),
        "friction_a": jnp.clip(jnp.exp(math.log(2.0) - 0.6931472 * jax.random.uniform(key_of[7], (ELEMENTS, NV), jnp.float32) ** level_of(key_of[7], (ELEMENTS, NV), ((0, 512),), -0.2, 0.2)), 1.0, 2.0),
        "heal_rate": jnp.clip(jnp.exp(math.log(0.5) - 1.609438 * jax.random.uniform(key_of[8], (ELEMENTS, NV), jnp.float32) ** level_of(key_of[8], (ELEMENTS, NV), ((0, 512),), -0.2, 0.2)), 0.1, 0.5),
    }


time_step = 0.25


def apply_kernel(leaves, near_flags, ranks, deviation):
    blocks = deviation.reshape(LEAVES, BLK, NV).astype(jnp.float32)
    rank_ids = jnp.arange(RMAX, dtype=jnp.int32)

    def one_row(item):
        leaf_row, near_row, rank_row, row_id = item
        columns = row_id + jnp.arange(3, dtype=jnp.int32) - 1
        valid = (columns >= 0) & (columns < LEAVES)
        safe_cols = jnp.clip(columns, 0, LEAVES - 1).astype(jnp.int32)
        band_leaves = leaf_row[safe_cols].astype(jnp.float32)
        band_blocks = blocks[safe_cols]
        band_near = (near_row[safe_cols] == 1) & valid
        dense = jnp.einsum("bij,bjn->bin", band_leaves, band_blocks)
        dense = jnp.sum(jnp.where(band_near[:, None, None], dense, 0.0), axis=0)
        factor_v = leaf_row[:, :, RMAX:].astype(jnp.float32)
        factor_u = leaf_row[:, :, :RMAX].astype(jnp.float32)
        inner = jnp.einsum("bjk,bjn->bkn", factor_v, blocks)
        keep_mask = (rank_ids[None, :] < rank_row[:, None]) & (near_row[:, None] == 0)
        inner = jnp.where(keep_mask[:, :, None], inner, 0.0).astype(jnp.bfloat16)
        inner = lax.optimization_barrier(inner).astype(jnp.float32)
        lowrank = jnp.einsum("bik,bkn->in", factor_u, inner)
        return dense + lowrank

    row_ids = jnp.arange(LEAVES, dtype=jnp.int32)
    result = lax.map(one_row, (leaves, near_flags, ranks, row_ids))
    return result.reshape(LEAVES * BLK, NV)


def reference(shear_leaves, normal_leaves, near_flags, ranks, shear_traction, normal_traction, state, friction_a, heal_rate):
    def rates(shear_now, normal_now, state_now):
        effective = jnp.maximum(normal_now, 1.0)
        slip_rate = 2.0 * jnp.exp(-state_now / friction_a) * jnp.sinh(shear_now / (friction_a * effective))
        deviation = (slip_rate - 1.0).astype(jnp.bfloat16)
        shear_rate = apply_kernel(shear_leaves, near_flags, ranks, deviation)
        normal_rate = apply_kernel(normal_leaves, near_flags, ranks, deviation)
        state_rate = heal_rate * (jnp.exp(-state_now) - slip_rate)
        return shear_rate, normal_rate, state_rate

    start = (shear_traction, normal_traction, state)
    first_rates = rates(*start)
    first = tuple(value + time_step * change for value, change in zip(start, first_rates))
    second_rates = rates(*first)
    second = tuple(0.75 * begin + 0.25 * (value + time_step * change) for begin, value, change in zip(start, first, second_rates))
    third_rates = rates(*second)
    third = tuple(begin / 3.0 + (2.0 / 3.0) * (value + time_step * change) for begin, value, change in zip(start, second, third_rates))
    return third[0], third[1], third[2]
```

```python
import functools
import math

import jax
import jax.numpy as jnp
from jax import lax
from jax.experimental import pallas as pl
from jax.experimental.pallas import tpu as pltpu
from jax.sharding import PartitionSpec as P

RMAX = 64
BLK = 128
XDIM = 4
MESH = pl.DeviceIdType.MESH
LN_HALF = math.log(0.5)

time_step = 0.25


def friction(shear_now, normal_now, state_now, friction_a):
    effective = jnp.maximum(normal_now, 1.0)
    ratio = shear_now / (friction_a * effective)
    sinh = jnp.exp(ratio + LN_HALF) - jnp.exp(LN_HALF - ratio)
    return 2.0 * jnp.exp(-state_now / friction_a) * sinh


def z_offsets(nz):
    far = [nz // 2]
    for dist in range(nz // 2 - 1, 0, -1):
        far += [dist, nz - dist]
    return far


def plane_offsets(ny):
    def dist(o):
        return min(o[0], ny - o[0]) + min(o[1], XDIM - o[1])

    every = [(dy, dx, dc) for dy in range(ny) for dx in range(XDIM) for dc in range(2)]
    return sorted([o for o in every if o != (0, 0, 0)], key=lambda o: -dist(o))


def kernel(
    nt, nz,
    near_ref, rank_ref, shear_leaf, normal_leaf, shear_in, normal_in, state_in, friction_in, heal_in,
    shear_out, normal_out, state_out,
    leaf_v, own_v, pack_send, pack_hold, block, xbuf, ybuf, pbuf,
    load_sem, zmove_send, zmove_recv, pmove_send, pmove_recv, x_send, x_recv, y_send, y_recv,
):
    ny = nt // 4
    rows = own_v.shape[1]
    t, s = lax.axis_index("tgt"), lax.axis_index("src")
    z, xhi = s // 2, s % 2
    y, xlo, core = t // 4, (t // 2) % 2, t % 2
    x = xhi * 2 + xlo
    me = t * 2 + xhi

    def z_peer(d):
        zt = (z + d) % nz
        return zt, (t, zt * 2 + xhi)

    def plane_peer(o):
        dy, dx, dc = o
        y2, x2, c2 = (y + dy) % ny, (x + dx) % XDIM, (core + dc) % 2
        t2, h2 = y2 * 4 + (x2 % 2) * 2 + c2, x2 // 2
        return t2 * 2 + h2, (t2, z * 2 + h2)

    zs, planes = z_offsets(nz), plane_offsets(ny)

    barrier = pltpu.get_barrier_semaphore()
    for d in zs:
        pl.semaphore_signal(barrier, inc=1, device_id=z_peer(d)[1], device_id_type=MESH)
    for o in planes:
        pl.semaphore_signal(barrier, inc=1, device_id=plane_peer(o)[1], device_id_type=MESH)

    loads = [
        pltpu.make_async_copy(src, own_v.at[i], load_sem.at[i])
        for i, src in enumerate((shear_in, normal_in, state_in, friction_in, heal_in))
    ] + [
        pltpu.make_async_copy(src.at[:, 0], leaf_v.at[i], load_sem.at[5 + i])
        for i, src in enumerate((shear_leaf, normal_leaf))
    ]
    for copy in loads:
        copy.start()
    for copy in loads[:5]:
        copy.wait()

    shear0, normal0, state0, fric, heal = (own_v[i] for i in range(5))

    slip = friction(shear0, normal0, state0, fric)
    xbuf[0, z] = (slip - 1.0).astype(jnp.bfloat16)

    for copy in loads[5:]:
        copy.wait()
    lane = lax.broadcasted_iota(jnp.int32, (BLK, BLK), 1)
    line = lax.broadcasted_iota(jnp.int32, (BLK, BLK), 0)
    dense = []
    for k in range(2):
        halves = []
        for h in range(2):
            leaf = leaf_v[k, h].astype(jnp.float32)
            u = jnp.where(lane < rank_ref[h, 0], leaf, 0.0).astype(jnp.bfloat16)
            v = pltpu.roll(leaf, RMAX, 1).astype(jnp.bfloat16)
            full = lax.dot_general(u, v, (((1,), (1,)), ((), ())), preferred_element_type=jnp.float32)
            halves.append(jnp.where(near_ref[h, 0] == 1, leaf, full).astype(jnp.bfloat16))
        dense.append(jnp.concatenate(halves, axis=0))
    shift = rows.bit_length() - 1
    inner = lane & (RMAX - 1)
    for h in range(2):
        column = ((inner >> shift) << (shift + 1)) + h * rows + (inner & (rows - 1))
        hit = line == column
        packed = 0.0
        for k in range(2):
            pick = jnp.where(hit & ((lane >> 6) == k), 1.0, 0.0).astype(jnp.bfloat16)
            packed = packed + jnp.dot(dense[k], pick, preferred_element_type=jnp.float32)
        pack_send[:, h] = packed.astype(jnp.bfloat16).reshape(nz, 2 * rows, BLK)
    pack_hold[z] = pack_send[z]

    pl.semaphore_wait(barrier, len(zs) + len(planes))

    def send_x(stage):
        for d in zs:
            pltpu.make_async_remote_copy(
                src_ref=xbuf.at[stage, z], dst_ref=xbuf.at[stage, z],
                send_sem=x_send.at[stage], recv_sem=x_recv.at[stage],
                device_id=z_peer(d)[1], device_id_type=MESH,
            ).start()

    def drain(view, sem):
        pltpu.make_async_copy(view, view, sem).wait()

    send_x(0)
    for d in zs:
        zt, peer = z_peer(d)
        pltpu.make_async_remote_copy(
            src_ref=pack_send.at[zt], dst_ref=pack_hold.at[z],
            send_sem=zmove_send, recv_sem=zmove_recv.at[z],
            device_id=peer, device_id_type=MESH,
        ).start()
    for d in [0] + zs[::-1]:
        z0 = (z + d) % nz
        if d:
            drain(pack_hold.at[z0], zmove_recv.at[z0])
        for dh in (1, 0):
            h = (xhi + dh) % 2

            def relay(z0=z0, h=h):
                pltpu.make_async_remote_copy(
                    src_ref=pack_hold.at[z0, h], dst_ref=block.at[xhi * nt + t],
                    send_sem=pmove_send, recv_sem=pmove_recv,
                    device_id=(z0, z * 2 + h), device_id_type=MESH,
                ).start()

            if dh:
                relay()
            else:
                pl.when(z0 != t)(relay)
    block[xhi * nt + t] = pack_hold[t, xhi]

    start = (shear0, normal0, state0)
    now = start
    for stage in range(3):
        if stage:
            slip = friction(now[0], now[1], now[2], fric)
            xbuf[stage, z] = (slip - 1.0).astype(jnp.bfloat16)
            send_x(stage)
        state_rate = heal * (jnp.exp(-now[2]) - slip)
        if stage == 0:
            drain(block.at[pl.ds(0, 2 * nt - 1)], pmove_recv)
        drain(xbuf.at[stage, pl.ds(0, nz - 1)], x_recv.at[stage])
        source = xbuf[stage].astype(jnp.float32).reshape(BLK, BLK)
        zero = jnp.zeros((RMAX, BLK), jnp.float32)
        low, high = source[:RMAX], source[RMAX:]
        left = jnp.concatenate([low, zero, high, zero], axis=0)
        right = jnp.concatenate([zero, low, zero, high], axis=0)
        rhs = jnp.concatenate([left, right], axis=1).astype(jnp.bfloat16)
        held = block[...].reshape(2, nt * 2 * rows, BLK)
        lhs = jnp.concatenate([held[0], held[1]], axis=1)
        product = jnp.dot(lhs, rhs, preferred_element_type=jnp.float32)
        for k in range(2):
            ybuf[stage, :, k] = product[:, k * BLK:(k + 1) * BLK].reshape(2 * nt, rows, BLK)
        for o in planes:
            q2, peer = plane_peer(o)
            pltpu.make_async_remote_copy(
                src_ref=ybuf.at[stage, q2], dst_ref=pbuf.at[stage, me],
                send_sem=y_send.at[stage], recv_sem=y_recv.at[stage],
                device_id=peer, device_id_type=MESH,
            ).start()
        pbuf[stage, me] = ybuf[stage, me]
        drain(pbuf.at[stage, pl.ds(0, 2 * nt - 1)], y_recv.at[stage])
        rate = jnp.sum(pbuf[stage], axis=0)
        changes = (rate[0], rate[1], state_rate)
        if stage == 0:
            now = tuple(v + time_step * c for v, c in zip(now, changes))
        elif stage == 1:
            now = tuple(0.75 * b + 0.25 * (v + time_step * c) for b, v, c in zip(start, now, changes))
        else:
            now = tuple(b / 3.0 + 2.0 / 3.0 * (v + time_step * c) for b, v, c in zip(start, now, changes))
    shear_out[...], normal_out[...], state_out[...] = now

    drain(pack_send.at[pl.ds(0, nz - 1)], zmove_send)
    drain(block.at[pl.ds(0, 2 * nt - 1)], pmove_send)
    for stage in range(3):
        drain(xbuf.at[stage, pl.ds(0, nz - 1)], x_send.at[stage])
        drain(ybuf.at[stage, pl.ds(0, 2 * nt - 1)], y_send.at[stage])


def solution(mesh):
    nt, ns = mesh.shape["tgt"], mesh.shape["src"]
    nz = ns // 2

    def step(shear_leaves, normal_leaves, near_flags, ranks, shear, normal, state, friction_a, heal_rate):
        rows, members = shear.shape
        out = jax.ShapeDtypeStruct((rows, members), jnp.float32)
        whole = pl.BlockSpec(memory_space=pl.ANY)
        scalars = pl.BlockSpec(memory_space=pltpu.SMEM)
        dma = pltpu.SemaphoreType.DMA
        return pl.pallas_call(
            functools.partial(kernel, nt, nz),
            out_shape=(out, out, out),
            in_specs=[scalars] * 2 + [whole] * 7,
            out_specs=[pl.BlockSpec(memory_space=pltpu.VMEM)] * 3,
            scratch_shapes=[
                pltpu.VMEM((2, 2, BLK, BLK), jnp.bfloat16),
                pltpu.VMEM((5, rows, members), jnp.float32),
                pltpu.VMEM((nz, 2, 2 * rows, BLK), jnp.bfloat16),
                pltpu.VMEM((nz, 2, 2 * rows, BLK), jnp.bfloat16),
                pltpu.VMEM((2 * nt, 2 * rows, BLK), jnp.bfloat16),
                pltpu.VMEM((3, nz, rows, members), jnp.bfloat16),
                pltpu.VMEM((3, 2 * nt, 2, rows, members), jnp.float32),
                pltpu.VMEM((3, 2 * nt, 2, rows, members), jnp.float32),
                dma((7,)), dma, dma((nz,)), dma, dma, dma((3,)), dma((3,)), dma((3,)), dma((3,)),
            ],
            compiler_params=pltpu.CompilerParams(collective_id=0, has_side_effects=True),
        )(near_flags, ranks, shear_leaves, normal_leaves, shear, normal, state, friction_a, heal_rate)

    both = P(("tgt", "src"), None)
    leaf = P("tgt", "src", None, None)
    flag = P("tgt", "src")
    return jax.shard_map(
        step, mesh=mesh, in_specs=(leaf, leaf, flag, flag) + (both,) * 5, out_specs=(both,) * 3, check_vma=False
    )
```

```python
import functools
import math

import jax
import jax.numpy as jnp
from jax import lax
from jax.experimental import pallas as pl
from jax.experimental.pallas import tpu as pltpu
from jax.sharding import PartitionSpec as P

RMAX = 64
BLK = 128
XDIM = 4
MESH = pl.DeviceIdType.MESH
LN_HALF = math.log(0.5)

VMEM_LIMIT = 16 * 2**20

time_step = 0.25


def friction(shear_now, normal_now, state_now, friction_a):
    effective = jnp.maximum(normal_now, 1.0)
    ratio = shear_now / (friction_a * effective)
    sinh = jnp.exp(ratio + LN_HALF) - jnp.exp(LN_HALF - ratio)
    return 2.0 * jnp.exp(-state_now / friction_a) * sinh


def z_offsets(nz):
    far = [nz // 2]
    for dist in range(nz // 2 - 1, 0, -1):
        far += [dist, nz - dist]
    return far


def plane_offsets(ny):
    def dist(o):
        return min(o[0], ny - o[0]) + min(o[1], XDIM - o[1])

    every = [(dy, dx, dc) for dy in range(ny) for dx in range(XDIM) for dc in range(2)]
    return sorted([o for o in every if o != (0, 0, 0)], key=lambda o: -dist(o))


def kernel(
    nt, nz,
    near_in, rank_in, shear_leaf, normal_leaf, shear_in, normal_in, state_in, friction_in, heal_in,
    done,
    near_ref, rank_ref, leaf_v, own_v, pack_send, pack_hold, block, held, xbuf, ybuf, pbuf,
    load_sem, zmove_send, zmove_recv, pmove_send, pmove_recv, x_send, x_recv, y_send, y_recv,
):
    ny = nt // 4
    rows = own_v.shape[1]
    t, s = lax.axis_index("tgt"), lax.axis_index("src")
    z, xhi = s // 2, s % 2
    y, xlo, core = t // 4, (t // 2) % 2, t % 2
    x = xhi * 2 + xlo
    chip = t // 2

    def z_peer(d, dc):
        zt = (z + d) % nz
        return zt, (chip * 2 + (core + dc) % 2, zt * 2 + xhi)

    def plane_peer(o):
        dy, dx, dc = o
        y2, x2, c2 = (y + dy) % ny, (x + dx) % XDIM, (core + dc) % 2
        t2, h2 = y2 * 4 + (x2 % 2) * 2 + c2, x2 // 2
        return t2 * 2 + h2, (t2, z * 2 + h2)

    zs, planes = z_offsets(nz), plane_offsets(ny)
    lines = [(d, dc) for d in zs for dc in (0, 1)] + [(0, 1)]

    barrier = pltpu.get_barrier_semaphore()
    for d, dc in lines[:-1]:
        pl.semaphore_signal(barrier, inc=1, device_id=z_peer(d, dc)[1], device_id_type=MESH)
    for o in planes:
        pl.semaphore_signal(barrier, inc=1, device_id=plane_peer(o)[1], device_id_type=MESH)

    loads = [
        pltpu.make_async_copy(src, own_v.at[i], load_sem.at[i])
        for i, src in enumerate((shear_in, normal_in, state_in, friction_in, heal_in))
    ] + [
        pltpu.make_async_copy(src.at[:, 0], leaf_v.at[i], load_sem.at[5 + i])
        for i, src in enumerate((shear_leaf, normal_leaf))
    ] + [
        pltpu.make_async_copy(near_in, near_ref, load_sem.at[7]),
        pltpu.make_async_copy(rank_in, rank_ref, load_sem.at[8]),
    ]
    for copy in loads:
        copy.start()
    for copy in loads[:5]:
        copy.wait()

    shear0, normal0, state0, fric, heal = (own_v[i] for i in range(5))

    slip = friction(shear0, normal0, state0, fric)
    xbuf[0, core * nz + z] = (slip - 1.0).astype(jnp.bfloat16)

    for copy in loads[5:]:
        copy.wait()
    lane = lax.broadcasted_iota(jnp.int32, (BLK, BLK), 1)
    line = lax.broadcasted_iota(jnp.int32, (BLK, BLK), 0)
    shift = rows.bit_length() - 1
    inner = lane & (RMAX - 1)
    hits = [line == ((inner >> shift) << (shift + 1)) + h * rows + (inner & (rows - 1)) for h in range(2)]
    picks = [
        [jnp.where(hit & ((lane >> 6) == g), 1.0, 0.0).astype(jnp.bfloat16) for g in range(2)] for hit in hits
    ]
    for k in range(2):
        halves = []
        for h in range(2):
            leaf = leaf_v[k, h].astype(jnp.float32)
            u = jnp.where(lane < rank_ref[0, h], leaf, 0.0).astype(jnp.bfloat16)
            v = pltpu.roll(leaf, RMAX, 1).astype(jnp.bfloat16)
            full = lax.dot_general(u, v, (((1,), (1,)), ((), ())), preferred_element_type=jnp.float32)
            halves.append(jnp.where(near_ref[0, h] == 1, leaf, full))
        dense = jnp.concatenate(halves, axis=0).reshape(nz, 2, rows, BLK)
        owners = [dense[:, g].reshape(BLK, BLK).astype(jnp.bfloat16) for g in range(2)]
        for h in range(2):
            packed = sum(jnp.dot(owners[g], picks[h][g], preferred_element_type=jnp.float32) for g in range(2))
            pack_send[:, k, h] = packed.reshape(nz, rows, BLK).astype(jnp.bfloat16)
    pack_hold[z // 2, :, :, z % 2] = pack_send[z]

    pl.semaphore_wait(barrier, len(lines) - 1 + len(planes))

    def send_x(stage):
        for d, dc in lines:
            pltpu.make_async_remote_copy(
                src_ref=xbuf.at[stage, core * nz + z], dst_ref=xbuf.at[stage, core * nz + z],
                send_sem=x_send.at[stage], recv_sem=x_recv.at[stage],
                device_id=z_peer(d, dc)[1], device_id_type=MESH,
            ).start()

    def drain(view, sem):
        pltpu.make_async_copy(view, view, sem).wait()

    for d in zs:
        zt, peer = z_peer(d, 0)
        pltpu.make_async_remote_copy(
            src_ref=pack_send.at[zt], dst_ref=pack_hold.at[z // 2, :, :, z % 2],
            send_sem=zmove_send, recv_sem=zmove_recv.at[z // 2],
            device_id=peer, device_id_type=MESH,
        ).start()
    send_x(0)
    near_first = [0]
    for dist in range(1, nz // 4):
        near_first += [dist, nz // 2 - dist]
    for dm in near_first + [nz // 4]:
        m0 = (z // 2 + dm) % (nz // 2)
        drain(pack_send.at[pl.ds(0, 2 if dm else 1)], zmove_recv.at[m0])
        for dk, dh in ((1, 1), (0, 1), (1, 0), (0, 0)):
            k, h = (core + dk) % 2, (xhi + dh) % 2

            def relay(m0=m0, k=k, h=h):
                pltpu.make_async_remote_copy(
                    src_ref=pack_hold.at[m0, k, h], dst_ref=block.at[xhi * nt + t],
                    send_sem=pmove_send, recv_sem=pmove_recv,
                    device_id=(m0 * 2 + k, z * 2 + h), device_id_type=MESH,
                ).start()

            if dk or dh:
                relay()
            else:
                pl.when(m0 != chip)(relay)
    block[xhi * nt + t] = pack_hold[chip, core, xhi]

    start = (shear0, normal0, state0)
    now = start
    zero = jnp.zeros((RMAX, BLK), jnp.float32)
    for stage in range(3):
        if stage:
            slip = friction(now[0], now[1], now[2], fric)
            xbuf[stage, core * nz + z] = (slip - 1.0).astype(jnp.bfloat16)
            send_x(stage)
        state_rate = heal * (jnp.exp(-now[2]) - slip)
        if stage == 0:
            drain(block.at[pl.ds(0, 2 * nt - 1)], pmove_recv)
            for i in range(4):
                b, g = i // 2, i % 2
                piece = block[g * nt:(g + 1) * nt, b].astype(jnp.float32)
                held[:, i * BLK:(i + 1) * BLK] = piece.reshape(BLK, BLK).astype(jnp.bfloat16)
        drain(xbuf.at[stage, pl.ds(0, 2 * nz - 1)], x_recv.at[stage])
        source = xbuf[stage].astype(jnp.float32).reshape(4, RMAX, BLK)
        left = jnp.concatenate([p for i in range(4) for p in (source[i], zero)], axis=0)
        right = jnp.concatenate([p for i in range(4) for p in (zero, source[i])], axis=0)
        rhs = jnp.concatenate([left, right], axis=1).astype(jnp.bfloat16)
        product = jnp.dot(held[...], rhs, preferred_element_type=jnp.float32)
        for g in range(2):
            ybuf[stage, :, g] = product[:, g * BLK:(g + 1) * BLK].reshape(nt, rows, BLK)
        mine = core * nt + chip * 2 + xhi
        for o in planes:
            q2, peer = plane_peer(o)
            pltpu.make_async_remote_copy(
                src_ref=ybuf.at[stage, q2 // 2, q2 % 2], dst_ref=pbuf.at[stage, mine],
                send_sem=y_send.at[stage], recv_sem=y_recv.at[stage],
                device_id=peer, device_id_type=MESH,
            ).start()
        pbuf[stage, mine] = ybuf[stage, t, xhi]
        drain(pbuf.at[stage, pl.ds(0, 2 * nt - 1)], y_recv.at[stage])
        changes = (jnp.sum(pbuf[stage, :nt], axis=0), jnp.sum(pbuf[stage, nt:], axis=0), state_rate)
        if stage == 0:
            now = tuple(v + time_step * c for v, c in zip(now, changes))
        elif stage == 1:
            now = tuple(0.75 * b + 0.25 * (v + time_step * c) for b, v, c in zip(start, now, changes))
        else:
            now = tuple(b / 3.0 + 2.0 / 3.0 * (v + time_step * c) for b, v, c in zip(start, now, changes))
    for i in range(3):
        done[i] = now[i]

    drain(pack_send.at[pl.ds(0, nz - 1)], zmove_send)
    drain(block.at[pl.ds(0, 2 * nt - 1)], pmove_send)
    for stage in range(3):
        drain(xbuf.at[stage, pl.ds(0, 2 * nz - 1)], x_send.at[stage])
        drain(pbuf.at[stage, pl.ds(0, 2 * nt - 1)], y_send.at[stage])


def store(done, shear_out, normal_out, state_out, sem):
    copies = [
        pltpu.make_async_copy(done.at[i], out, sem.at[i]) for i, out in enumerate((shear_out, normal_out, state_out))
    ]
    for copy in copies:
        copy.start()
    for copy in copies:
        copy.wait()


def solution(mesh):
    nt, ns = mesh.shape["tgt"], mesh.shape["src"]
    nz = ns // 2

    def step(shear_leaves, normal_leaves, near_flags, ranks, shear, normal, state, friction_a, heal_rate):
        rows, members = shear.shape
        out = jax.ShapeDtypeStruct((rows, members), jnp.float32)
        whole = pl.BlockSpec(memory_space=pltpu.HBM)
        dma = pltpu.SemaphoreType.DMA
        done = pl.pallas_call(
            functools.partial(kernel, nt, nz),
            out_shape=jax.ShapeDtypeStruct((3, rows, members), jnp.float32),
            in_specs=[whole] * 9,
            out_specs=pl.BlockSpec(memory_space=pltpu.VMEM),
            scratch_shapes=[
                pltpu.SMEM((1, 2), jnp.int32),
                pltpu.SMEM((1, 2), jnp.int32),
                pltpu.VMEM((2, 2, BLK, BLK), jnp.bfloat16),
                pltpu.VMEM((5, rows, members), jnp.float32),
                pltpu.VMEM((nz, 2, 2, rows, BLK), jnp.bfloat16),
                pltpu.VMEM((nz // 2, 2, 2, 2, rows, BLK), jnp.bfloat16),
                pltpu.VMEM((2 * nt, 2, rows, BLK), jnp.bfloat16),
                pltpu.VMEM((BLK, 4 * BLK), jnp.bfloat16),
                pltpu.VMEM((3, 2 * nz, rows, members), jnp.bfloat16),
                pltpu.VMEM((3, nt, 2, rows, members), jnp.float32),
                pltpu.VMEM((3, 2 * nt, rows, members), jnp.float32),
                dma((9,)), dma, dma((nz // 2,)), dma, dma, dma((3,)), dma((3,)), dma((3,)), dma((3,)),
            ],
            compiler_params=pltpu.CompilerParams(
                collective_id=0, has_side_effects=True, vmem_limit_bytes=VMEM_LIMIT
            ),
        )(
            *(pltpu.with_memory_space_constraint(v, pltpu.HBM) for v in (
                near_flags.reshape(1, 2), ranks.reshape(1, 2),
                shear_leaves, normal_leaves, shear, normal, state, friction_a, heal_rate,
            )),
        )
        return pl.pallas_call(
            store,
            out_shape=(out, out, out),
            in_specs=[pl.BlockSpec(memory_space=pltpu.VMEM)],
            out_specs=[whole] * 3,
            scratch_shapes=[dma((3,))],
            compiler_params=pltpu.CompilerParams(vmem_limit_bytes=2**20),
        )(done)

    both = P(("tgt", "src"), None)
    leaf = P("tgt", "src", None, None)
    flag = P("tgt", "src")
    return jax.shard_map(
        step, mesh=mesh, in_specs=(leaf, leaf, flag, flag) + (both,) * 5, out_specs=(both,) * 3, check_vma=False
    )
```

```python
import functools
import math

import jax
import jax.numpy as jnp
from jax import lax
from jax.experimental import pallas as pl
from jax.experimental.pallas import tpu as pltpu
from jax.sharding import PartitionSpec as P

RMAX = 64
BLK = 128
XDIM = 4
MESH = pl.DeviceIdType.MESH
LN_HALF = math.log(0.5)

VMEM_LIMIT = 16 * 2**20

time_step = 0.25


def friction(shear_now, normal_now, state_now, friction_a):
    effective = jnp.maximum(normal_now, 1.0)
    ratio = shear_now / (friction_a * effective)
    sinh = jnp.exp(ratio + LN_HALF) - jnp.exp(LN_HALF - ratio)
    return 2.0 * jnp.exp(-state_now / friction_a) * sinh


def z_offsets(nz):
    far = [nz // 2]
    for dist in range(nz // 2 - 1, 0, -1):
        far += [dist, nz - dist]
    return far


def plane_offsets(ny):
    def dist(o):
        return min(o[0], ny - o[0]) + min(o[1], XDIM - o[1])

    every = [(dy, dx, dc) for dy in range(ny) for dx in range(XDIM) for dc in range(2)]
    return sorted([o for o in every if o != (0, 0, 0)], key=lambda o: -dist(o))


def kernel(
    nt, nz,
    near_in, rank_in, shear_leaf, normal_leaf, shear_in, normal_in, state_in, friction_in, heal_in,
    done,
    near_ref, rank_ref, leaf_v, own_v, pack_send, pack_hold, block, held, xbuf, ybuf, pbuf,
    load_sem, fwd_send, fwd_recv, zmove_send, zmove_recv, pmove_send, pmove_recv, x_send, x_recv, y_send, y_recv,
):
    ny = nt // 4
    rows = own_v.shape[1]
    t, s = lax.axis_index("tgt"), lax.axis_index("src")
    z, xhi = s // 2, s % 2
    y, xlo, core = t // 4, (t // 2) % 2, t % 2
    x = xhi * 2 + xlo
    chip = t // 2

    def z_peer(d, dc):
        zt = (z + d) % nz
        return zt, (chip * 2 + (core + dc) % 2, zt * 2 + xhi)

    def plane_peer(o):
        dy, dx, dc = o
        y2, x2, c2 = (y + dy) % ny, (x + dx) % XDIM, (core + dc) % 2
        t2, h2 = y2 * 4 + (x2 % 2) * 2 + c2, x2 // 2
        return t2 * 2 + h2, (t2, z * 2 + h2)

    zs, planes = z_offsets(nz), plane_offsets(ny)
    lines = [(d, dc) for d in zs for dc in (0, 1)] + [(0, 1)]

    barrier = pltpu.get_barrier_semaphore()
    for d, dc in lines[:-1]:
        pl.semaphore_signal(barrier, inc=1, device_id=z_peer(d, dc)[1], device_id_type=MESH)
    for o in planes:
        pl.semaphore_signal(barrier, inc=1, device_id=plane_peer(o)[1], device_id_type=MESH)

    loads = [
        pltpu.make_async_copy(src, own_v.at[i], load_sem.at[i])
        for i, src in enumerate((shear_in, normal_in, state_in, friction_in, heal_in))
    ] + [
        pltpu.make_async_copy(src.at[:, 0], leaf_v.at[i], load_sem.at[5 + i])
        for i, src in enumerate((shear_leaf, normal_leaf))
    ] + [
        pltpu.make_async_copy(near_in, near_ref, load_sem.at[7]),
        pltpu.make_async_copy(rank_in, rank_ref, load_sem.at[8]),
    ]
    for copy in loads:
        copy.start()
    for copy in loads[:5]:
        copy.wait()

    shear0, normal0, state0, fric, heal = (own_v[i] for i in range(5))

    slip = friction(shear0, normal0, state0, fric)
    xbuf[0, core * nz + z] = (slip - 1.0).astype(jnp.bfloat16)

    for copy in loads[5:]:
        copy.wait()
    lane = lax.broadcasted_iota(jnp.int32, (BLK, BLK), 1)
    line = lax.broadcasted_iota(jnp.int32, (BLK, BLK), 0)
    shift = rows.bit_length() - 1
    inner = lane & (RMAX - 1)
    hits = [line == ((inner >> shift) << (shift + 1)) + h * rows + (inner & (rows - 1)) for h in range(2)]
    picks = [
        [jnp.where(hit & ((lane >> 6) == g), 1.0, 0.0).astype(jnp.bfloat16) for g in range(2)] for hit in hits
    ]
    for k in range(2):
        halves = []
        for h in range(2):
            leaf = leaf_v[k, h].astype(jnp.float32)
            u = jnp.where(lane < rank_ref[0, h], leaf, 0.0).astype(jnp.bfloat16)
            v = pltpu.roll(leaf, RMAX, 1).astype(jnp.bfloat16)
            full = lax.dot_general(u, v, (((1,), (1,)), ((), ())), preferred_element_type=jnp.float32)
            halves.append(jnp.where(near_ref[0, h] == 1, leaf, full))
        dense = jnp.concatenate(halves, axis=0).reshape(nz, 2, rows, BLK)
        owners = [dense[:, g].reshape(BLK, BLK).astype(jnp.bfloat16) for g in range(2)]
        for h in range(2):
            packed = sum(jnp.dot(owners[g], picks[h][g], preferred_element_type=jnp.float32) for g in range(2))
            pack_send[:, k, h] = packed.reshape(nz, rows, BLK).astype(jnp.bfloat16)
    pack_hold[z // 2, :, :, z % 2] = pack_send[z]

    pl.semaphore_wait(barrier, len(lines) - 1 + len(planes))

    def send_x(stage):
        for d, dc in lines if stage else lines[:-1:2]:
            pltpu.make_async_remote_copy(
                src_ref=xbuf.at[stage, core * nz + z], dst_ref=xbuf.at[stage, core * nz + z],
                send_sem=x_send.at[stage], recv_sem=x_recv.at[stage],
                device_id=z_peer(d, dc)[1], device_id_type=MESH,
            ).start()

    def drain(view, sem):
        pltpu.make_async_copy(view, view, sem).wait()

    for d in zs:
        zt, peer = z_peer(d, 0)
        pltpu.make_async_remote_copy(
            src_ref=pack_send.at[zt], dst_ref=pack_hold.at[z // 2, :, :, z % 2],
            send_sem=zmove_send, recv_sem=zmove_recv.at[z // 2],
            device_id=peer, device_id_type=MESH,
        ).start()
    send_x(0)
    near_first = [0]
    for dist in range(1, nz // 4):
        near_first += [dist, nz // 2 - dist]
    for dm in near_first + [nz // 4]:
        m0 = (z // 2 + dm) % (nz // 2)
        drain(pack_send.at[pl.ds(0, 2 if dm else 1)], zmove_recv.at[m0])
        for dk, dh in ((1, 1), (0, 1), (1, 0), (0, 0)):
            k, h = (core + dk) % 2, (xhi + dh) % 2

            def relay(m0=m0, k=k, h=h):
                pltpu.make_async_remote_copy(
                    src_ref=pack_hold.at[m0, k, h], dst_ref=block.at[xhi * nt + t],
                    send_sem=pmove_send, recv_sem=pmove_recv,
                    device_id=(m0 * 2 + k, z * 2 + h), device_id_type=MESH,
                ).start()

            if dk or dh:
                relay()
            else:
                pl.when(m0 != chip)(relay)
    block[xhi * nt + t] = pack_hold[chip, core, xhi]
    drain(xbuf.at[0, pl.ds(0, nz - 1)], x_recv.at[0])
    column = xbuf.at[0, pl.ds(core * nz, nz)]
    forward = pltpu.make_async_remote_copy(
        src_ref=column, dst_ref=column, send_sem=fwd_send, recv_sem=fwd_recv,
        device_id=z_peer(0, 1)[1], device_id_type=MESH,
    )
    forward.start()

    start = (shear0, normal0, state0)
    now = start
    zero = jnp.zeros((RMAX, BLK), jnp.float32)
    for stage in range(3):
        if stage:
            slip = friction(now[0], now[1], now[2], fric)
            xbuf[stage, core * nz + z] = (slip - 1.0).astype(jnp.bfloat16)
            send_x(stage)
        state_rate = heal * (jnp.exp(-now[2]) - slip)
        if stage == 0:
            drain(block.at[pl.ds(0, 2 * nt - 1)], pmove_recv)
            for i in range(4):
                b, g = i // 2, i % 2
                piece = block[g * nt:(g + 1) * nt, b].astype(jnp.float32)
                held[:, i * BLK:(i + 1) * BLK] = piece.reshape(BLK, BLK).astype(jnp.bfloat16)
            forward.wait_recv()
        else:
            drain(xbuf.at[stage, pl.ds(0, 2 * nz - 1)], x_recv.at[stage])
        source = xbuf[stage].astype(jnp.float32).reshape(4, RMAX, BLK)
        left = jnp.concatenate([p for i in range(4) for p in (source[i], zero)], axis=0)
        right = jnp.concatenate([p for i in range(4) for p in (zero, source[i])], axis=0)
        rhs = jnp.concatenate([left, right], axis=1).astype(jnp.bfloat16)
        product = jnp.dot(held[...], rhs, preferred_element_type=jnp.float32)
        for g in range(2):
            ybuf[stage, :, g] = product[:, g * BLK:(g + 1) * BLK].reshape(nt, rows, BLK)
        mine = core * nt + chip * 2 + xhi
        for o in planes:
            q2, peer = plane_peer(o)
            pltpu.make_async_remote_copy(
                src_ref=ybuf.at[stage, q2 // 2, q2 % 2], dst_ref=pbuf.at[stage, mine],
                send_sem=y_send.at[stage], recv_sem=y_recv.at[stage],
                device_id=peer, device_id_type=MESH,
            ).start()
        pbuf[stage, mine] = ybuf[stage, t, xhi]
        drain(pbuf.at[stage, pl.ds(0, 2 * nt - 1)], y_recv.at[stage])
        changes = (jnp.sum(pbuf[stage, :nt], axis=0), jnp.sum(pbuf[stage, nt:], axis=0), state_rate)
        if stage == 0:
            now = tuple(v + time_step * c for v, c in zip(now, changes))
        elif stage == 1:
            now = tuple(0.75 * b + 0.25 * (v + time_step * c) for b, v, c in zip(start, now, changes))
        else:
            now = tuple(b / 3.0 + 2.0 / 3.0 * (v + time_step * c) for b, v, c in zip(start, now, changes))
    for i in range(3):
        done[i] = now[i]

    drain(pack_send.at[pl.ds(0, nz - 1)], zmove_send)
    drain(block.at[pl.ds(0, 2 * nt - 1)], pmove_send)
    forward.wait_send()
    for stage in range(3):
        drain(xbuf.at[stage, pl.ds(0, 2 * nz - 1 if stage else nz - 1)], x_send.at[stage])
        drain(pbuf.at[stage, pl.ds(0, 2 * nt - 1)], y_send.at[stage])


def store(done, shear_out, normal_out, state_out, sem):
    copies = [
        pltpu.make_async_copy(done.at[i], out, sem.at[i]) for i, out in enumerate((shear_out, normal_out, state_out))
    ]
    for copy in copies:
        copy.start()
    for copy in copies:
        copy.wait()


def solution(mesh):
    nt, ns = mesh.shape["tgt"], mesh.shape["src"]
    nz = ns // 2

    def step(shear_leaves, normal_leaves, near_flags, ranks, shear, normal, state, friction_a, heal_rate):
        rows, members = shear.shape
        out = jax.ShapeDtypeStruct((rows, members), jnp.float32)
        whole = pl.BlockSpec(memory_space=pltpu.HBM)
        dma = pltpu.SemaphoreType.DMA
        done = pl.pallas_call(
            functools.partial(kernel, nt, nz),
            out_shape=jax.ShapeDtypeStruct((3, rows, members), jnp.float32),
            in_specs=[whole] * 9,
            out_specs=pl.BlockSpec(memory_space=pltpu.VMEM),
            scratch_shapes=[
                pltpu.SMEM((1, 2), jnp.int32),
                pltpu.SMEM((1, 2), jnp.int32),
                pltpu.VMEM((2, 2, BLK, BLK), jnp.bfloat16),
                pltpu.VMEM((5, rows, members), jnp.float32),
                pltpu.VMEM((nz, 2, 2, rows, BLK), jnp.bfloat16),
                pltpu.VMEM((nz // 2, 2, 2, 2, rows, BLK), jnp.bfloat16),
                pltpu.VMEM((2 * nt, 2, rows, BLK), jnp.bfloat16),
                pltpu.VMEM((BLK, 4 * BLK), jnp.bfloat16),
                pltpu.VMEM((3, 2 * nz, rows, members), jnp.bfloat16),
                pltpu.VMEM((3, nt, 2, rows, members), jnp.float32),
                pltpu.VMEM((3, 2 * nt, rows, members), jnp.float32),
                dma((9,)), dma, dma, dma, dma((nz // 2,)), dma, dma, dma((3,)), dma((3,)), dma((3,)), dma((3,)),
            ],
            compiler_params=pltpu.CompilerParams(
                collective_id=0, has_side_effects=True, vmem_limit_bytes=VMEM_LIMIT
            ),
        )(
            *(pltpu.with_memory_space_constraint(v, pltpu.HBM) for v in (
                near_flags.reshape(1, 2), ranks.reshape(1, 2),
                shear_leaves, normal_leaves, shear, normal, state, friction_a, heal_rate,
            )),
        )
        return pl.pallas_call(
            store,
            out_shape=(out, out, out),
            in_specs=[pl.BlockSpec(memory_space=pltpu.VMEM)],
            out_specs=[whole] * 3,
            scratch_shapes=[dma((3,))],
            compiler_params=pltpu.CompilerParams(vmem_limit_bytes=2**20),
        )(done)

    both = P(("tgt", "src"), None)
    leaf = P("tgt", "src", None, None)
    flag = P("tgt", "src")
    return jax.shard_map(
        step, mesh=mesh, in_specs=(leaf, leaf, flag, flag) + (both,) * 5, out_specs=(both,) * 3, check_vma=False
    )
```

```python
import functools
import math

import jax
import jax.numpy as jnp
from jax import lax
from jax.experimental import pallas as pl
from jax.experimental.pallas import tpu as pltpu
from jax.sharding import PartitionSpec as P

RMAX = 64
BLK = 128
XDIM = 4
MESH = pl.DeviceIdType.MESH
LN_HALF = math.log(0.5)

VMEM_LIMIT = 16 * 2**20

time_step = 0.25


def friction(shear_now, normal_now, state_now, friction_a):
    effective = jnp.maximum(normal_now, 1.0)
    ratio = shear_now / (friction_a * effective)
    sinh = jnp.exp(ratio + LN_HALF) - jnp.exp(LN_HALF - ratio)
    return 2.0 * jnp.exp(-state_now / friction_a) * sinh


def z_offsets(nz):
    far = [nz // 2]
    for dist in range(nz // 2 - 1, 0, -1):
        far += [dist, nz - dist]
    return far


def plane_offsets(ny):
    def dist(o):
        return min(o[0], ny - o[0]) + min(o[1], XDIM - o[1])

    every = [(dy, dx, dc) for dy in range(ny) for dx in range(XDIM) for dc in range(2)]
    return sorted([o for o in every if o != (0, 0, 0)], key=lambda o: -dist(o))


def kernel(
    nt, nz,
    near_in, rank_in, shear_leaf, normal_leaf, shear_in, normal_in, state_in, friction_in, heal_in,
    done,
    near_ref, rank_ref, leaf_v, own_v, pack_send, pack_hold, block, held, xbuf, ybuf, pbuf,
    load_sem, fwd_send, fwd_recv, zmove_send, zmove_recv, pmove_send, pmove_recv, x_send, x_recv, x_near, y_send, y_recv,
):
    ny = nt // 4
    rows, members = own_v.shape[1:]
    t, s = lax.axis_index("tgt"), lax.axis_index("src")
    z, xhi = lax.div(s, 2), lax.rem(s, 2)
    y, xlo, core = lax.div(t, 4), lax.rem(lax.div(t, 2), 2), lax.rem(t, 2)
    x = xhi * 2 + xlo
    chip = lax.div(t, 2)

    def z_peer(d, dc):
        zt = lax.rem(z + d, nz)
        return zt, (chip * 2 + lax.rem(core + dc, 2), zt * 2 + xhi)

    def plane_peer(o):
        dy, dx, dc = o
        y2, x2, c2 = lax.rem(y + dy, ny), lax.rem(x + dx, XDIM), lax.rem(core + dc, 2)
        t2, h2 = y2 * 4 + lax.rem(x2, 2) * 2 + c2, lax.div(x2, 2)
        return t2 * 2 + h2, (t2, z * 2 + h2)

    zs, planes = z_offsets(nz), plane_offsets(ny)
    lines = [(d, dc) for d in zs for dc in (0, 1)] + [(0, 1)]
    close = [(d, 0) for d in zs if min(d, nz - d) <= nz // 4]
    short = [l for l in lines if (l[0], 0) not in close or l[1] == 0]

    barrier = pltpu.get_barrier_semaphore()
    for d, dc in lines[:-1]:
        pl.semaphore_signal(barrier, inc=1, device_id=z_peer(d, dc)[1], device_id_type=MESH)
    for o in planes:
        pl.semaphore_signal(barrier, inc=1, device_id=plane_peer(o)[1], device_id_type=MESH)

    loads = [
        pltpu.make_async_copy(src, own_v.at[i], load_sem.at[i])
        for i, src in enumerate((shear_in, normal_in, state_in, friction_in, heal_in))
    ] + [
        pltpu.make_async_copy(src.at[:, 0], leaf_v.at[i], load_sem.at[5 + i])
        for i, src in enumerate((shear_leaf, normal_leaf))
    ] + [
        pltpu.make_async_copy(near_in, near_ref, load_sem.at[7]),
        pltpu.make_async_copy(rank_in, rank_ref, load_sem.at[8]),
    ]
    for copy in loads:
        copy.start()
    for copy in loads[:5]:
        copy.wait()

    shear0, normal0, state0, fric, heal = (own_v[i] for i in range(5))

    slip = friction(shear0, normal0, state0, fric)
    xbuf[0, core * nz + z] = (slip - 1.0).astype(jnp.bfloat16)

    for copy in loads[5:]:
        copy.wait()
    lane = lax.broadcasted_iota(jnp.int32, (BLK, BLK), 1)
    line = lax.broadcasted_iota(jnp.int32, (BLK, BLK), 0)
    shift = rows.bit_length() - 1
    inner = lane & (RMAX - 1)
    hits = [line == ((inner >> shift) << (shift + 1)) + h * rows + (inner & (rows - 1)) for h in range(2)]
    picks = [
        [jnp.where(hit & ((lane >> 6) == g), 1.0, 0.0).astype(jnp.bfloat16) for g in range(2)] for hit in hits
    ]
    for k in range(2):
        halves = []
        for h in range(2):
            leaf = leaf_v[k, h].astype(jnp.float32)
            u = jnp.where(lane < rank_ref[0, h], leaf, 0.0).astype(jnp.bfloat16)
            v = pltpu.roll(leaf, RMAX, 1).astype(jnp.bfloat16)
            full = lax.dot_general(u, v, (((1,), (1,)), ((), ())), preferred_element_type=jnp.float32)
            halves.append(jnp.where(near_ref[0, h] == 1, leaf, full))
        dense = jnp.concatenate(halves, axis=0).reshape(nz, 2, rows, BLK)
        owners = [dense[:, g].reshape(BLK, BLK).astype(jnp.bfloat16) for g in range(2)]
        for h in range(2):
            packed = sum(jnp.dot(owners[g], picks[h][g], preferred_element_type=jnp.float32) for g in range(2))
            pack_send[:, k, h] = packed.reshape(nz, rows, BLK).astype(jnp.bfloat16)
    pack_hold[lax.div(z, 2), :, :, lax.rem(z, 2)] = pack_send[z]

    pl.semaphore_wait(barrier, len(lines) - 1 + len(planes))

    def drain(view, sem):
        pltpu.make_async_copy(view, view, sem).wait()

    def send_x(stage):
        for d, dc in short if stage else lines[:-1:2]:
            recv = x_near if stage and (d, dc) in close else x_recv
            pltpu.make_async_remote_copy(
                src_ref=xbuf.at[stage, core * nz + z], dst_ref=xbuf.at[stage, core * nz + z],
                send_sem=x_send.at[stage], recv_sem=recv.at[stage],
                device_id=z_peer(d, dc)[1], device_id_type=MESH,
            ).start()
        if stage:
            drain(xbuf.at[stage, pl.ds(0, len(close))], x_near.at[stage])
            for d, _ in close:
                zt, _ = z_peer(d, 0)
                pltpu.make_async_remote_copy(
                    src_ref=xbuf.at[stage, core * nz + zt], dst_ref=xbuf.at[stage, core * nz + zt],
                    send_sem=x_send.at[stage], recv_sem=x_recv.at[stage],
                    device_id=z_peer(0, 1)[1], device_id_type=MESH,
                ).start()

    for d in zs:
        zt, peer = z_peer(d, 0)
        pltpu.make_async_remote_copy(
            src_ref=pack_send.at[zt], dst_ref=pack_hold.at[lax.div(z, 2), :, :, lax.rem(z, 2)],
            send_sem=zmove_send, recv_sem=zmove_recv.at[lax.div(z, 2)],
            device_id=peer, device_id_type=MESH,
        ).start()
    send_x(0)
    near_first = [0]
    for dist in range(1, nz // 4):
        near_first += [dist, nz // 2 - dist]
    for dm in near_first + [nz // 4]:
        m0 = lax.rem(lax.div(z, 2) + dm, nz // 2)
        drain(pack_send.at[pl.ds(0, 2 if dm else 1)], zmove_recv.at[m0])
        for dk, dh in ((1, 1), (0, 1), (1, 0), (0, 0)):
            k, h = lax.rem(core + dk, 2), lax.rem(xhi + dh, 2)

            def relay(m0=m0, k=k, h=h):
                pltpu.make_async_remote_copy(
                    src_ref=pack_hold.at[m0, k, h], dst_ref=block.at[xhi * nt + t],
                    send_sem=pmove_send, recv_sem=pmove_recv,
                    device_id=(m0 * 2 + k, z * 2 + h), device_id_type=MESH,
                ).start()

            if dk or dh:
                relay()
            else:
                pl.when(m0 != chip)(relay)
    block[xhi * nt + t] = pack_hold[chip, core, xhi]
    drain(xbuf.at[0, pl.ds(0, nz - 1)], x_recv.at[0])
    column = xbuf.at[0, pl.ds(core * nz, nz)]
    forward = pltpu.make_async_remote_copy(
        src_ref=column, dst_ref=column, send_sem=fwd_send, recv_sem=fwd_recv,
        device_id=z_peer(0, 1)[1], device_id_type=MESH,
    )
    forward.start()

    start = (shear0, normal0, state0)
    now = start
    for stage in range(3):
        if stage:
            slip = friction(now[0], now[1], now[2], fric)
            xbuf[stage, core * nz + z] = (slip - 1.0).astype(jnp.bfloat16)
            send_x(stage)
        state_rate = heal * (jnp.exp(-now[2]) - slip)
        if stage == 0:
            drain(block.at[pl.ds(0, 2 * nt - 1)], pmove_recv)
            for b in range(2):
                low, high = (
                    block[g * nt:(g + 1) * nt, b].astype(jnp.float32).reshape(BLK, BLK) for g in range(2)
                )
                spot = pl.ds(b * BLK, BLK)
                held[:BLK, spot] = jnp.where(lane < RMAX, low, pltpu.roll(high, RMAX, 1)).astype(jnp.bfloat16)
                held[BLK:, spot] = jnp.where(lane < RMAX, pltpu.roll(low, RMAX, 1), high).astype(jnp.bfloat16)
            forward.wait_recv()
        else:
            drain(xbuf.at[stage, pl.ds(0, 2 * nz - 1 - len(close))], x_recv.at[stage])
        source = xbuf[stage].astype(jnp.float32).reshape(2 * BLK, members).astype(jnp.bfloat16)
        product = jnp.dot(held[...], source, preferred_element_type=jnp.float32)
        for g in range(2):
            ybuf[stage, :, g] = product[g * BLK:(g + 1) * BLK].reshape(nt, rows, members)
        mine = core * nt + chip * 2 + xhi
        for o in planes:
            q2, peer = plane_peer(o)
            pltpu.make_async_remote_copy(
                src_ref=ybuf.at[stage, lax.div(q2, 2), lax.rem(q2, 2)], dst_ref=pbuf.at[stage, mine],
                send_sem=y_send.at[stage], recv_sem=y_recv.at[stage],
                device_id=peer, device_id_type=MESH,
            ).start()
        pbuf[stage, mine] = ybuf[stage, t, xhi]
        drain(pbuf.at[stage, pl.ds(0, 2 * nt - 1)], y_recv.at[stage])
        changes = (jnp.sum(pbuf[stage, :nt], axis=0), jnp.sum(pbuf[stage, nt:], axis=0), state_rate)
        if stage == 0:
            now = tuple(v + time_step * c for v, c in zip(now, changes))
        elif stage == 1:
            now = tuple(0.75 * b + 0.25 * (v + time_step * c) for b, v, c in zip(start, now, changes))
        else:
            now = tuple(b / 3.0 + 2.0 / 3.0 * (v + time_step * c) for b, v, c in zip(start, now, changes))
    for i in range(3):
        done[i] = now[i]

    drain(pack_send.at[pl.ds(0, nz - 1)], zmove_send)
    drain(block.at[pl.ds(0, 2 * nt - 1)], pmove_send)
    forward.wait_send()
    for stage in range(3):
        drain(xbuf.at[stage, pl.ds(0, 2 * nz - 1 if stage else nz - 1)], x_send.at[stage])
        drain(pbuf.at[stage, pl.ds(0, 2 * nt - 1)], y_send.at[stage])


def store(done, shear_out, normal_out, state_out, sem):
    copies = [
        pltpu.make_async_copy(done.at[i], out, sem.at[i]) for i, out in enumerate((shear_out, normal_out, state_out))
    ]
    for copy in copies:
        copy.start()
    for copy in copies:
        copy.wait()


def solution(mesh):
    nt, ns = mesh.shape["tgt"], mesh.shape["src"]
    nz = ns // 2

    def step(shear_leaves, normal_leaves, near_flags, ranks, shear, normal, state, friction_a, heal_rate):
        rows, members = shear.shape
        out = jax.ShapeDtypeStruct((rows, members), jnp.float32)
        whole = pl.BlockSpec(memory_space=pltpu.HBM)
        dma = pltpu.SemaphoreType.DMA
        done = pl.pallas_call(
            functools.partial(kernel, nt, nz),
            out_shape=jax.ShapeDtypeStruct((3, rows, members), jnp.float32),
            in_specs=[whole] * 9,
            out_specs=pl.BlockSpec(memory_space=pltpu.VMEM),
            scratch_shapes=[
                pltpu.SMEM((1, 2), jnp.int32),
                pltpu.SMEM((1, 2), jnp.int32),
                pltpu.VMEM((2, 2, BLK, BLK), jnp.bfloat16),
                pltpu.VMEM((5, rows, members), jnp.float32),
                pltpu.VMEM((nz, 2, 2, rows, BLK), jnp.bfloat16),
                pltpu.VMEM((nz // 2, 2, 2, 2, rows, BLK), jnp.bfloat16),
                pltpu.VMEM((2 * nt, 2, rows, BLK), jnp.bfloat16),
                pltpu.VMEM((2 * BLK, 2 * BLK), jnp.bfloat16),
                pltpu.VMEM((3, 2 * nz, rows, members), jnp.bfloat16),
                pltpu.VMEM((3, nt, 2, rows, members), jnp.float32),
                pltpu.VMEM((3, 2 * nt, rows, members), jnp.float32),
                dma((9,)), dma, dma, dma, dma((nz // 2,)), dma, dma, dma((3,)), dma((3,)), dma((3,)), dma((3,)), dma((3,)),
            ],
            compiler_params=pltpu.CompilerParams(
                collective_id=0, has_side_effects=True,
                vmem_limit_bytes=VMEM_LIMIT
            ),
        )(
            *(pltpu.with_memory_space_constraint(v, pltpu.HBM) for v in (
                near_flags.reshape(1, 2), ranks.reshape(1, 2),
                shear_leaves, normal_leaves, shear, normal, state, friction_a, heal_rate,
            )),
        )
        return pl.pallas_call(
            store,
            out_shape=(out, out, out),
            in_specs=[pl.BlockSpec(memory_space=pltpu.VMEM)],
            out_specs=[whole] * 3,
            scratch_shapes=[dma((3,))],
            compiler_params=pltpu.CompilerParams(vmem_limit_bytes=2**20),
        )(done)

    both = P(("tgt", "src"), None)
    leaf = P("tgt", "src", None, None)
    flag = P("tgt", "src")
    return jax.shard_map(
        step, mesh=mesh, in_specs=(leaf, leaf, flag, flag) + (both,) * 5, out_specs=(both,) * 3, check_vma=False
    )
```

```python
import functools
import math

import jax
import jax.numpy as jnp
from jax import lax
from jax.experimental import pallas as pl
from jax.experimental.pallas import tpu as pltpu
from jax.sharding import PartitionSpec as P

RMAX = 64
BLK = 128
XDIM = 4
MESH = pl.DeviceIdType.MESH
LN_HALF = math.log(0.5)

VMEM_LIMIT = 16 * 2**20

time_step = 0.25


def friction(shear_now, normal_now, state_now, friction_a):
    effective = jnp.maximum(normal_now, 1.0)
    ratio = shear_now / (friction_a * effective)
    sinh = jnp.exp(ratio + LN_HALF) - jnp.exp(LN_HALF - ratio)
    return 2.0 * jnp.exp(-state_now / friction_a) * sinh


def z_offsets(nz):
    far = [nz // 2]
    for dist in range(nz // 2 - 1, 0, -1):
        far += [dist, nz - dist]
    return far


def plane_offsets(ny):
    def dist(o):
        return min(o[0], ny - o[0]) + min(o[1], XDIM - o[1])

    every = [(dy, dx, dc) for dy in range(ny) for dx in range(XDIM) for dc in range(2)]
    return sorted([o for o in every if o != (0, 0, 0)], key=lambda o: -dist(o))


def kernel(
    nt, nz,
    near_in, rank_in, shear_leaf, normal_leaf, shear_in, normal_in, state_in, friction_in, heal_in,
    done,
    near_ref, rank_ref, leaf_v, own_v, pack_send, pack_hold, block, held, xbuf, ybuf, pbuf,
    load_sem, fwd_send, fwd_recv, zmove_send, zmove_recv, pmove_send, pmove_recv, x_send, x_recv, x_near, y_send, y_recv,
):
    ny = nt // 4
    rows, members = own_v.shape[1:]
    t, s = lax.axis_index("tgt"), lax.axis_index("src")
    z, xhi = lax.div(s, 2), lax.rem(s, 2)
    y, xlo, core = lax.div(t, 4), lax.rem(lax.div(t, 2), 2), lax.rem(t, 2)
    x = xhi * 2 + xlo
    chip = lax.div(t, 2)

    def z_peer(d, dc):
        zt = lax.rem(z + d, nz)
        return zt, (chip * 2 + lax.rem(core + dc, 2), zt * 2 + xhi)

    def plane_peer(o):
        dy, dx, dc = o
        y2, x2, c2 = lax.rem(y + dy, ny), lax.rem(x + dx, XDIM), lax.rem(core + dc, 2)
        t2, h2 = y2 * 4 + lax.rem(x2, 2) * 2 + c2, lax.div(x2, 2)
        return t2 * 2 + h2, (t2, z * 2 + h2)

    zs, planes = z_offsets(nz), plane_offsets(ny)
    lines = [(d, dc) for d in zs for dc in (0, 1)] + [(0, 1)]
    close = [(d, 0) for d in zs if min(d, nz - d) <= nz // 4]
    short = [l for l in lines if (l[0], 0) not in close or l[1] == 0]

    barrier = pltpu.get_barrier_semaphore()
    for d in zs:
        pl.semaphore_signal(barrier, inc=1, device_id=z_peer(d, 0)[1], device_id_type=MESH)
    for o in planes:
        pl.semaphore_signal(barrier, inc=1, device_id=plane_peer(o)[1], device_id_type=MESH)

    loads = [
        pltpu.make_async_copy(src, own_v.at[i], load_sem.at[i])
        for i, src in enumerate((shear_in, normal_in, state_in, friction_in, heal_in))
    ] + [
        pltpu.make_async_copy(src.at[:, 0], leaf_v.at[i], load_sem.at[5 + i])
        for i, src in enumerate((shear_leaf, normal_leaf))
    ] + [
        pltpu.make_async_copy(near_in, near_ref, load_sem.at[7]),
        pltpu.make_async_copy(rank_in, rank_ref, load_sem.at[8]),
    ]
    for copy in loads:
        copy.start()
    for copy in loads[:5]:
        copy.wait()

    shear0, normal0, state0, fric, heal = (own_v[i] for i in range(5))

    slip = friction(shear0, normal0, state0, fric)
    xbuf[0, core * nz + z] = (slip - 1.0).astype(jnp.bfloat16)

    for copy in loads[5:]:
        copy.wait()
    lane = lax.broadcasted_iota(jnp.int32, (BLK, BLK), 1)
    line = lax.broadcasted_iota(jnp.int32, (BLK, BLK), 0)
    shift = rows.bit_length() - 1
    inner = lane & (RMAX - 1)
    hits = [line == ((inner >> shift) << (shift + 1)) + h * rows + (inner & (rows - 1)) for h in range(2)]
    picks = [
        [jnp.where(hit & ((lane >> 6) == g), 1.0, 0.0).astype(jnp.bfloat16) for g in range(2)] for hit in hits
    ]
    for k in range(2):
        halves = []
        for h in range(2):
            leaf = leaf_v[k, h].astype(jnp.float32)
            u = jnp.where(lane < rank_ref[0, h], leaf, 0.0).astype(jnp.bfloat16)
            v = pltpu.roll(leaf, RMAX, 1).astype(jnp.bfloat16)
            full = lax.dot_general(u, v, (((1,), (1,)), ((), ())), preferred_element_type=jnp.float32)
            halves.append(jnp.where(near_ref[0, h] == 1, leaf, full))
        dense = jnp.concatenate(halves, axis=0).reshape(nz, 2, rows, BLK)
        owners = [dense[:, g].reshape(BLK, BLK).astype(jnp.bfloat16) for g in range(2)]
        for h in range(2):
            packed = sum(jnp.dot(owners[g], picks[h][g], preferred_element_type=jnp.float32) for g in range(2))
            pack_send[:, k, h] = packed.reshape(nz, rows, BLK).astype(jnp.bfloat16)
    pack_hold[lax.div(z, 2), :, :, lax.rem(z, 2)] = pack_send[z]

    pl.semaphore_wait(barrier, len(zs) + len(planes))

    def drain(view, sem):
        pltpu.make_async_copy(view, view, sem).wait()

    def send_x(stage):
        for d, dc in short if stage else lines[:-1:2]:
            recv = x_near if stage and (d, dc) in close else x_recv
            pltpu.make_async_remote_copy(
                src_ref=xbuf.at[stage, core * nz + z], dst_ref=xbuf.at[stage, core * nz + z],
                send_sem=x_send.at[stage], recv_sem=recv.at[stage],
                device_id=z_peer(d, dc)[1], device_id_type=MESH,
            ).start()
        if stage:
            drain(xbuf.at[stage, pl.ds(0, len(close))], x_near.at[stage])
            for d, _ in close:
                zt, _ = z_peer(d, 0)
                pltpu.make_async_remote_copy(
                    src_ref=xbuf.at[stage, core * nz + zt], dst_ref=xbuf.at[stage, core * nz + zt],
                    send_sem=x_send.at[stage], recv_sem=x_recv.at[stage],
                    device_id=z_peer(0, 1)[1], device_id_type=MESH,
                ).start()

    for d in zs:
        zt, peer = z_peer(d, 0)
        pltpu.make_async_remote_copy(
            src_ref=pack_send.at[zt], dst_ref=pack_hold.at[lax.div(z, 2), :, :, lax.rem(z, 2)],
            send_sem=zmove_send, recv_sem=zmove_recv.at[lax.div(z, 2)],
            device_id=peer, device_id_type=MESH,
        ).start()
    send_x(0)
    near_first = [0]
    for dist in range(1, nz // 4):
        near_first += [dist, nz // 2 - dist]
    for dm in near_first + [nz // 4]:
        m0 = lax.rem(lax.div(z, 2) + dm, nz // 2)
        drain(pack_send.at[pl.ds(0, 2 if dm else 1)], zmove_recv.at[m0])
        for dk, dh in ((1, 1), (0, 1), (1, 0), (0, 0)):
            k, h = lax.rem(core + dk, 2), lax.rem(xhi + dh, 2)

            def relay(m0=m0, k=k, h=h):
                pltpu.make_async_remote_copy(
                    src_ref=pack_hold.at[m0, k, h], dst_ref=block.at[xhi * nt + t],
                    send_sem=pmove_send, recv_sem=pmove_recv,
                    device_id=(m0 * 2 + k, z * 2 + h), device_id_type=MESH,
                ).start()

            if dk or dh:
                relay()
            else:
                pl.when(m0 != chip)(relay)
    block[xhi * nt + t] = pack_hold[chip, core, xhi]
    drain(xbuf.at[0, pl.ds(0, nz - 1)], x_recv.at[0])
    column = xbuf.at[0, pl.ds(core * nz, nz)]
    forward = pltpu.make_async_remote_copy(
        src_ref=column, dst_ref=column, send_sem=fwd_send, recv_sem=fwd_recv,
        device_id=z_peer(0, 1)[1], device_id_type=MESH,
    )
    forward.start()

    start = (shear0, normal0, state0)
    now = start
    for stage in range(3):
        if stage:
            slip = friction(now[0], now[1], now[2], fric)
            xbuf[stage, core * nz + z] = (slip - 1.0).astype(jnp.bfloat16)
            send_x(stage)
        state_rate = heal * (jnp.exp(-now[2]) - slip)
        if stage == 0:
            drain(block.at[pl.ds(0, 2 * nt - 1)], pmove_recv)
            for b in range(2):
                low, high = (
                    block[g * nt:(g + 1) * nt, b].astype(jnp.float32).reshape(BLK, BLK) for g in range(2)
                )
                spot = pl.ds(b * BLK, BLK)
                held[:BLK, spot] = jnp.where(lane < RMAX, low, pltpu.roll(high, RMAX, 1)).astype(jnp.bfloat16)
                held[BLK:, spot] = jnp.where(lane < RMAX, pltpu.roll(low, RMAX, 1), high).astype(jnp.bfloat16)
            forward.wait_recv()
        else:
            drain(xbuf.at[stage, pl.ds(0, 2 * nz - 1 - len(close))], x_recv.at[stage])
        source = xbuf[stage].astype(jnp.float32).reshape(2 * BLK, members).astype(jnp.bfloat16)
        product = jnp.dot(held[...], source, preferred_element_type=jnp.float32)
        for g in range(2):
            ybuf[stage, :, g] = product[g * BLK:(g + 1) * BLK].reshape(nt, rows, members)
        mine = core * nt + chip * 2 + xhi
        for o in planes:
            q2, peer = plane_peer(o)
            pltpu.make_async_remote_copy(
                src_ref=ybuf.at[stage, lax.div(q2, 2), lax.rem(q2, 2)], dst_ref=pbuf.at[stage, mine],
                send_sem=y_send.at[stage], recv_sem=y_recv.at[stage],
                device_id=peer, device_id_type=MESH,
            ).start()
        pbuf[stage, mine] = ybuf[stage, t, xhi]
        drain(pbuf.at[stage, pl.ds(0, 2 * nt - 1)], y_recv.at[stage])
        changes = (jnp.sum(pbuf[stage, :nt], axis=0), jnp.sum(pbuf[stage, nt:], axis=0), state_rate)
        if stage == 0:
            now = tuple(v + time_step * c for v, c in zip(now, changes))
        elif stage == 1:
            now = tuple(0.75 * b + 0.25 * (v + time_step * c) for b, v, c in zip(start, now, changes))
        else:
            now = tuple(b / 3.0 + 2.0 / 3.0 * (v + time_step * c) for b, v, c in zip(start, now, changes))
    for i in range(3):
        done[i] = now[i]

    drain(pack_send.at[pl.ds(0, nz - 1)], zmove_send)
    drain(block.at[pl.ds(0, 2 * nt - 1)], pmove_send)
    forward.wait_send()
    for stage in range(3):
        drain(xbuf.at[stage, pl.ds(0, 2 * nz - 1 if stage else nz - 1)], x_send.at[stage])
        drain(pbuf.at[stage, pl.ds(0, 2 * nt - 1)], y_send.at[stage])


def store(done, shear_out, normal_out, state_out, sem):
    copies = [
        pltpu.make_async_copy(done.at[i], out, sem.at[i]) for i, out in enumerate((shear_out, normal_out, state_out))
    ]
    for copy in copies:
        copy.start()
    for copy in copies:
        copy.wait()


def solution(mesh):
    nt, ns = mesh.shape["tgt"], mesh.shape["src"]
    nz = ns // 2

    def step(shear_leaves, normal_leaves, near_flags, ranks, shear, normal, state, friction_a, heal_rate):
        rows, members = shear.shape
        out = jax.ShapeDtypeStruct((rows, members), jnp.float32)
        whole = pl.BlockSpec(memory_space=pltpu.HBM)
        dma = pltpu.SemaphoreType.DMA
        done = pl.pallas_call(
            functools.partial(kernel, nt, nz),
            out_shape=jax.ShapeDtypeStruct((3, rows, members), jnp.float32),
            in_specs=[whole] * 9,
            out_specs=pl.BlockSpec(memory_space=pltpu.VMEM),
            scratch_shapes=[
                pltpu.SMEM((1, 2), jnp.int32),
                pltpu.SMEM((1, 2), jnp.int32),
                pltpu.VMEM((2, 2, BLK, BLK), jnp.bfloat16),
                pltpu.VMEM((5, rows, members), jnp.float32),
                pltpu.VMEM((nz, 2, 2, rows, BLK), jnp.bfloat16),
                pltpu.VMEM((nz // 2, 2, 2, 2, rows, BLK), jnp.bfloat16),
                pltpu.VMEM((2 * nt, 2, rows, BLK), jnp.bfloat16),
                pltpu.VMEM((2 * BLK, 2 * BLK), jnp.bfloat16),
                pltpu.VMEM((3, 2 * nz, rows, members), jnp.bfloat16),
                pltpu.VMEM((3, nt, 2, rows, members), jnp.float32),
                pltpu.VMEM((3, 2 * nt, rows, members), jnp.float32),
                dma((9,)), dma, dma, dma, dma((nz // 2,)), dma, dma, dma((3,)), dma((3,)), dma((3,)), dma((3,)), dma((3,)),
            ],
            compiler_params=pltpu.CompilerParams(
                collective_id=0, has_side_effects=True,
                vmem_limit_bytes=VMEM_LIMIT
            ),
        )(
            *(pltpu.with_memory_space_constraint(v, pltpu.HBM) for v in (
                near_flags.reshape(1, 2), ranks.reshape(1, 2),
                shear_leaves, normal_leaves, shear, normal, state, friction_a, heal_rate,
            )),
        )
        return pl.pallas_call(
            store,
            out_shape=(out, out, out),
            in_specs=[pl.BlockSpec(memory_space=pltpu.VMEM)],
            out_specs=[whole] * 3,
            scratch_shapes=[dma((3,))],
            compiler_params=pltpu.CompilerParams(vmem_limit_bytes=2**20),
        )(done)

    both = P(("tgt", "src"), None)
    leaf = P("tgt", "src", None, None)
    flag = P("tgt", "src")
    return jax.shard_map(
        step, mesh=mesh, in_specs=(leaf, leaf, flag, flag) + (both,) * 5, out_specs=(both,) * 3, check_vma=False
    )
```
